512 devices in a mesh: limb: 16 (over x_hi, z), coef: 32 (over x_lo, y, core).
Axes of the slice: x: 4 (x_hi: 2, x_lo: 2; x = x_hi * 2 + x_lo), y: 8, z: 8, core: 2. Of those that a mesh axis runs over, the one named last changes fastest.
Arguments:
- cipher_zero: float32 [24, 32, 65536], P(None, 'limb', 'coef'), may hold values from -6 to 6
- cipher_one: float32 [24, 32, 65536], P(None, 'limb', 'coef'), may hold values from -6 to 6
- key_main: bfloat16 [24, 2, 2, 32, 65536], P(None, None, None, 'limb', 'coef'), may hold values from -5 to 5
- key_special: bfloat16 [24, 2, 2, 16, 65536], P(None, None, None, 'limb', 'coef'), may hold values from -5 to 5
- lift_main: float32 [32, 32], replicated, may hold values from -1.5 to 1.5
- lift_special: float32 [32, 16], replicated, may hold values from -1.5 to 1.5
- lower_table: float32 [16, 32], replicated, may hold values from -1.5 to 1.5
- inverse_scale: float32 [32], P('limb'), may hold values from 0.5 to 1.5
- inverse_main: float32 [32, 256, 256], P('limb', 'coef'), may hold values from 0.5 to 1.5
- inverse_special: float32 [16, 256, 256], P('limb', 'coef'), may hold values from 0.5 to 1.5
- forward_main: float32 [32, 256, 256], P('limb', 'coef'), may hold values from 0.5 to 1.5
- forward_special: float32 [16, 256, 256], P('limb', 'coef'), may hold values from 0.5 to 1.5
- inverse_rows: float32 [256, 256], replicated, may hold values from -0.375 to 0.375
- inverse_columns: float32 [256, 256], replicated, may hold values from -0.375 to 0.375
- forward_rows: float32 [256, 256], replicated, may hold values from -0.375 to 0.375
- forward_columns: float32 [256, 256], replicated, may hold values from -0.375 to 0.375
Outputs:
- switched_zero: float32 [24, 32, 65536], P(None, 'limb', 'coef')
- switched_one: float32 [24, 32, 65536], P(None, 'limb', 'coef')
The draws below stay inside these ranges and needn't reach their ends.
All inputs are finite; a program needn't handle non-finite values.
Results may differ from the reference program's by a relative error of at most 0.0003.
Values sent between devices are 32-bit elements; how exact they have to be, the bound alone decides.
A program may use at most 64 MiB of HBM per device.

```python
import jax
import jax.numpy as jnp
from jax import lax

CT = 24
L = 32
K = 16
ROWS = 256
COLS = 256
DIGITS = 2
N = 65536


def shard_levels(key, dims, pieces, least, high):
    factor_of, own = 1.0, jax.random.fold_in(key, 6)
    for dim, blocks in pieces:
        heights = jnp.exp(jax.random.uniform(jax.random.fold_in(own, dim), (blocks,), jnp.float32, least / len(pieces), high / len(pieces)))
        factor_of = factor_of * jnp.repeat(heights, dims[dim] // blocks).reshape([-1 if axis == dim else 1 for axis in range(len(dims))])
    return factor_of


def noise(key, shape, deviation, most, shards=(), kind=jnp.bfloat16):
    entries = jax.random.normal(key, shape, jnp.float32) * deviation
    if len(shards) > 0:
        entries = shard_levels(key, shape, shards, -0.22, 0.18) * entries
    return jnp.clip(entries, min=-most, max=most).astype(kind)


def setup_inputs(seed: int = 0) -> dict:
    seeds = jax.random.split(jax.random.key(seed), 17)
    return {
        "cipher_zero": noise(seeds[0], (CT, L, N), 1.0, 6.0, ((1, 16), (2, 32)), jnp.float32),
        "cipher_one": noise(seeds[1], (CT, L, N), 1.0, 6.0, ((1, 16), (2, 32)), jnp.float32),
        "key_main": noise(seeds[2], (CT, DIGITS, 2, L, N), 0.7, 5.0, ((3, 16), (4, 32))),
        "key_special": noise(seeds[3], (CT, DIGITS, 2, K, N), 0.7, 5.0, ((3, 16), (4, 32))),
        "lift_main": noise(seeds[4], (L, L), K ** -0.5, 1.5, (), jnp.float32),
        "lift_special": noise(seeds[5], (L, K), K ** -0.5, 1.5, (), jnp.float32),
        "lower_table": noise(seeds[6], (K, L), K ** -0.5, 1.5, (), jnp.float32),
        "inverse_scale": jnp.clip(0.5 + 1.0 * jax.random.uniform(seeds[7], (L,), jnp.float32) ** shard_levels(seeds[7], (L,), ((0, 16),), -0.2, 0.2), 0.5, 1.5),
        "inverse_main": jnp.clip(0.5 + 1.0 * jax.random.uniform(seeds[8], (L, ROWS, COLS), jnp.float32) ** shard_levels(seeds[8], (L, ROWS, COLS), ((0, 16), (1, 32)), -0.2, 0.2), 0.5, 1.5),
        "inverse_special": jnp.clip(0.5 + 1.0 * jax.random.uniform(seeds[9], (K, ROWS, COLS), jnp.float32) ** shard_levels(seeds[9], (K, ROWS, COLS), ((0, 16), (1, 32)), -0.2, 0.2), 0.5, 1.5),
        "forward_main": jnp.clip(0.5 + 1.0 * jax.random.uniform(seeds[10], (L, COLS, ROWS), jnp.float32) ** shard_levels(seeds[10], (L, COLS, ROWS), ((0, 16), (1, 32)), -0.2, 0.2), 0.5, 1.5),
        "forward_special": jnp.clip(0.5 + 1.0 * jax.random.uniform(seeds[11], (K, COLS, ROWS), jnp.float32) ** shard_levels(seeds[11], (K, COLS, ROWS), ((0, 16), (1, 32)), -0.2, 0.2), 0.5, 1.5),
        "inverse_rows": noise(seeds[12], (ROWS, ROWS), ROWS ** -0.5, 0.375, (), jnp.float32),
        "inverse_columns": noise(seeds[13], (COLS, COLS), COLS ** -0.5, 0.375, (), jnp.float32),
        "forward_rows": noise(seeds[14], (ROWS, ROWS), ROWS ** -0.5, 0.375, (), jnp.float32),
        "forward_columns": noise(seeds[15], (COLS, COLS), COLS ** -0.5, 0.375, (), jnp.float32),
    }


HIGHEST = lax.Precision.HIGHEST


def inverse_four(values, twiddle, inverse_rows, inverse_columns):
    partial_value = jnp.einsum("...rc,ck->...rk", values, inverse_columns, precision=HIGHEST) * twiddle
    return jnp.einsum("...rk,rj->...kj", partial_value, inverse_rows, precision=HIGHEST)


def forward_four(coeffs, twiddle, forward_rows, forward_columns):
    partial_value = jnp.einsum("...cr,rk->...ck", coeffs, forward_rows, precision=HIGHEST) * twiddle
    return jnp.einsum("...ck,cm->...km", partial_value, forward_columns, precision=HIGHEST)


def reference(cipher_zero, cipher_one, key_main, key_special, lift_main, lift_special, lower_table, inverse_scale, inverse_main, inverse_special, forward_main, forward_special, inverse_rows, inverse_columns, forward_rows, forward_columns):
    digits = L // K
    owner = (jnp.arange(L) // K)[None, :] == jnp.arange(digits)[:, None]
    digit_mask = owner.astype(lift_main.dtype)
    masked_main = digit_mask[:, :, None] * lift_main[None]
    masked_special = digit_mask[:, :, None] * lift_special[None]

    def single(record):
        first_part, second_part, keys_main, keys_special = record
        coeffs = inverse_four(second_part.reshape(L, ROWS, COLS), inverse_main, inverse_rows, inverse_columns).reshape(L, ROWS * COLS)
        lifted_main = jnp.einsum("sn,dst->dtn", coeffs, masked_main, precision=HIGHEST)
        lifted_sp = jnp.einsum("sn,dst->dtn", coeffs, masked_special, precision=HIGHEST)
        values_main = forward_four(lifted_main.reshape(digits, L, COLS, ROWS), forward_main, forward_rows, forward_columns).reshape(digits, L, ROWS * COLS)
        values_sp = forward_four(lifted_sp.reshape(digits, K, COLS, ROWS), forward_special, forward_rows, forward_columns).reshape(digits, K, ROWS * COLS)
        summed_main = jnp.sum(values_main[:, None] * keys_main.astype(values_main.dtype), axis=0)
        summed_sp = jnp.sum(values_sp[:, None] * keys_special.astype(values_sp.dtype), axis=0)
        special = inverse_four(summed_sp.reshape(2, K, ROWS, COLS), inverse_special, inverse_rows, inverse_columns).reshape(2, K, ROWS * COLS)
        lowered = jnp.einsum("sjn,jt->stn", special, lower_table, precision=HIGHEST)
        lowered = forward_four(lowered.reshape(2, L, COLS, ROWS), forward_main, forward_rows, forward_columns).reshape(2, L, ROWS * COLS)
        result = inverse_scale[:, None] * (summed_main - lowered)
        return first_part + result[0], result[1]

    switched_zero, switched_one = lax.map(single, (cipher_zero, cipher_one, key_main, key_special))
    return switched_zero, switched_one
```

```python
import functools

import jax
import jax.numpy as jnp
from jax import lax
from jax.experimental import pallas as pl
from jax.experimental.pallas import tpu as pltpu
from jax.sharding import PartitionSpec as P

F32, BF16 = jnp.float32, jnp.bfloat16
HIGHEST = lax.Precision.HIGHEST
MESH = pl.DeviceIdType.MESH
ROWS = COLS = 256
SUB, LANE = 8, 128
PART = 8
ORDER_SKEW = 1.0


def halves(v):
    high = v.astype(BF16)
    return high, (v - high.astype(F32)).astype(BF16)


def iota(shape, axis):
    return lax.broadcasted_iota(jnp.int32, shape, axis)


def selector(shape, condition):
    return jnp.where(condition(iota(shape, 0), iota(shape, 1)), 1.0, 0.0).astype(F32)


def exact(a, b, dims):
    return lax.dot_general(a, b, (dims, ((), ())), precision=HIGHEST, preferred_element_type=F32)


def fold(a, b):
    return jnp.dot(a, b, preferred_element_type=F32)


def data_rows(v):
    high, low = halves(v)
    return jnp.concatenate([high, high, low], axis=1)


def data_columns(v):
    high, low = halves(v)
    return jnp.concatenate([high, high, low], axis=0)


def weight_right(v):
    high, low = halves(v)
    return jnp.concatenate([high, low, high], axis=0)


def weight_left(v):
    high, low = halves(v)
    return jnp.concatenate([high, low, high], axis=1)


def kernel(
    coef_size, limb_size, chunks,
    x_ref, zero_ref, km_ref, ks_ref, lift_main_ref, lift_special_ref, lower_ref, scale_ref,
    tim_ref, tis_ref, tfm_ref, tfs_ref, ir_ref, ic_ref, fr_ref, fc_ref,
    out0_ref, out1_ref,
    send1, got1, send2, got2, got3, send4, got4, send5, got5, send6, got6, got7, send8, got8,
    send_t, got_t, twist, total, ic_w, fc_w, m_w, lift_w, lower_w,
    ssem, rsem, tsem,
):
    coef = lax.axis_index("coef")
    limb = lax.axis_index("limb")
    ring = limb_size // 2
    side = limb // ring
    place = lax.rem(limb, ring)

    barrier = pltpu.get_barrier_semaphore()

    @pl.loop(1, coef_size)
    def _(j):
        pl.semaphore_signal(barrier, inc=1, device_id={"coef": lax.rem(coef + j, coef_size)}, device_id_type=MESH)

    @pl.loop(1, limb_size)
    def _(j):
        pl.semaphore_signal(barrier, inc=1, device_id={"limb": lax.rem(limb + j, limb_size)}, device_id_type=MESH)

    def push(source, target, axis, peer, stage, g):
        pltpu.make_async_remote_copy(
            src_ref=source, dst_ref=target, send_sem=ssem.at[stage, g], recv_sem=rsem.at[stage, g],
            device_id={axis: peer}, device_id_type=MESH,
        ).start()

    def settle(ref, sem):
        pltpu.make_async_copy(ref, ref, sem).wait()

    def coef_push(send, got, stage, g):
        @pl.loop(1, coef_size)
        def _(j):
            peer = lax.rem(coef + j, coef_size)
            push(send.at[g, peer], got.at[g, coef], "coef", peer, stage, g)

        got[g, coef] = send[g, coef]

    def coef_wait(got, stage, g):
        settle(got.at[g, pl.ds(0, coef_size - 1)], rsem.at[stage, g])

    def to_items(ref, g, v):
        for n in range(v.shape[0]):
            for h in range(2):
                ref[g, 2 * n + h] = v[n, :, h * LANE:(h + 1) * LANE]

    def stage1(g):
        v = x_ref[pl.ds(PART * g, PART)].reshape(PART * 2 * SUB, COLS)
        a = fold(data_rows(v), ic_w[...]).reshape(PART, 2, SUB, COLS) * tim_ref[...][None]
        to_items(send1, g, a.reshape(PART * 2, SUB, COLS))

    def push1(g):
        coef_push(send1, got1, 0, g)

    def stage2(g):
        coef_wait(got1, 0, g)
        v = got1[g].reshape(ROWS, LANE)
        send2[g] = fold(m_w[...], data_columns(v)).reshape(coef_size, SUB, LANE)
        coef_push(send2, got2, 1, g)

    def stage3(g):
        coef_wait(got2, 1, g)

        @pl.loop(1, ring)
        def _(j):
            to = lax.rem(place + j, ring)
            push(got2.at[g, pl.ds(4 * to, 4)], got3.at[g, place], "limb", side * ring + to, 2, g)

        got3[g, place] = got2[g, pl.ds(4 * place, 4)]

    def mixed(weight, got, send, stage, per, g, wait_count, wait_stage):
        settle(got.at[g, pl.ds(0, wait_count)], rsem.at[wait_stage, g])
        v = got[g].reshape(limb_size, 2, SUB, LANE)
        both = jnp.concatenate(
            [v[:, 0].reshape(limb_size * SUB, LANE), v[:, 1].reshape(limb_size * SUB, LANE)], axis=1
        )
        w = fold(weight[...], data_columns(both)).reshape(limb_size, per, SUB, 2 * LANE)
        for h in range(2):
            send[g, :, :, h] = w[..., h * LANE:(h + 1) * LANE]

    def limb_push(send, got, stage, g):
        @pl.loop(1, limb_size)
        def _(j):
            peer = lax.rem(limb + j, limb_size)
            push(send.at[g, peer], got.at[g, limb], "limb", peer, stage, g)

        got[g, limb] = send[g, limb]

    def stage4(g):
        mixed(lift_w, got3, send4, 3, 3, g, ring - 1, 2)
        limb_push(send4, got4, 3, g)

    def finish(v, kinds, n):
        parts = [(v[:, :, h] * twist[:kinds, h][None]).reshape(n * kinds * SUB, LANE) for h in range(2)]
        rows = jnp.concatenate(parts, axis=1)
        return fold(data_rows(rows), fc_w[...]).reshape(n, kinds * SUB, COLS)

    def stage5(g):
        settle(got4.at[g, pl.ds(0, limb_size - 1)], rsem.at[3, g])
        values = finish(got4[g], 3, limb_size).reshape(2, PART, 3 * SUB, COLS)
        here = pl.ds(PART * g, PART)
        for i in range(2):
            total[g, :, i] = sum(
                values[d, :, :2 * SUB] * km_ref[here, d, i].astype(F32) for d in range(2)
            )
        special = 0.0
        for d in range(2):
            v = values[d, :, 2 * SUB:]
            special = special + jnp.concatenate([v, v], axis=1) * ks_ref[here, d].astype(F32)
        a = fold(data_rows(special.reshape(PART * 2 * SUB, COLS)), ic_w[...])
        a = a.reshape(PART * 2, SUB, COLS) * tis_ref[...]
        to_items(send5, g, a)
        coef_push(send5, got5, 4, g)

    def stage6(g):
        coef_wait(got5, 4, g)
        v = got5[g].reshape(ROWS, LANE)
        send6[g] = fold(m_w[...], data_columns(v)).reshape(coef_size, SUB, LANE)
        coef_push(send6, got6, 5, g)

    def stage7(g):
        coef_wait(got6, 5, g)

        @pl.loop(1, limb_size)
        def _(j):
            to = lax.rem(limb + j, limb_size)
            push(got6.at[g, pl.ds(2 * to, 2)], got7.at[g, limb], "limb", to, 6, g)

        got7[g, limb] = got6[g, pl.ds(2 * limb, 2)]

    def stage8(g):
        mixed(lower_w, got7, send8, 7, 2, g, limb_size - 1, 6)
        limb_push(send8, got8, 7, g)

    def stage9(g):
        settle(got8.at[g, pl.ds(0, limb_size - 1)], rsem.at[7, g])
        low = finish(got8[g], 2, limb_size).reshape(PART, 2, 2, SUB, COLS)
        here = pl.ds(PART * g, PART)
        for t in range(2):
            for i, out in enumerate((out0_ref, out1_ref)):
                result = scale_ref[t] * (total[g, :, i, t * SUB:(t + 1) * SUB] - low[:, i, t])
                out[here, t] = zero_ref[here, t] + result if i == 0 else result

    def prepare_twist():
        rows = jnp.concatenate(
            [tfm_ref[...].reshape(2 * SUB, ROWS), tfs_ref[...].reshape(SUB, ROWS), jnp.zeros((LANE - 3 * SUB, ROWS), F32)],
            axis=0,
        )
        send_t[...] = rows.T.reshape(coef_size, SUB, LANE)

    def push_twist():
        @pl.loop(1, coef_size)
        def _(j):
            peer = lax.rem(coef + j, coef_size)
            pltpu.make_async_remote_copy(
                src_ref=send_t.at[peer], dst_ref=got_t.at[coef], send_sem=tsem.at[0], recv_sem=tsem.at[1],
                device_id={"coef": peer}, device_id_type=MESH,
            ).start()

        got_t[coef] = send_t[coef]

    def build_twist():
        settle(got_t.at[pl.ds(0, coef_size - 1)], tsem.at[1])
        lanes = iota((SUB, LANE), 1) // SUB
        per = LANE // SUB
        for t in range(3):
            for h in range(2):
                value = jnp.zeros((SUB, LANE), F32)
                for q in range(per):
                    tile = got_t[h * per + q]
                    shift = (q - t) * SUB % LANE
                    moved = pltpu.roll(tile, shift, 1) if shift else tile
                    value = jnp.where(lanes == q, moved, value)
                twist[t, h] = value

    def build_weights():
        m_w[...] = weight_left(exact(fr_ref[...], ir_ref[...], ((0,), (1,))))
        fc_w[...] = weight_right(fc_ref[...])

    def build_mixes():
        depth = limb_size * SUB
        spread = selector((limb_size, depth), lambda s, c: c // SUB == s)
        mine = pl.ds(pl.multiple_of(side * limb_size, SUB), limb_size)

        def expand(table, rows):
            wide = exact(table, spread, ((1,), (0,)))
            keep = lax.rem(iota((rows, depth), 0), SUB) == lax.rem(iota((rows, depth), 1), SUB)
            return weight_left(jnp.where(keep, wide, 0.0))

        rows = limb_size * 3 * SUB
        kinds = limb_size * 2

        def main_of(r, t):
            which = r // SUB
            return (lax.rem(which, 3) < 2) & (2 * (which // 3) + lax.rem(which, 3) == t)

        def special_of(r, u):
            which = r // SUB
            return (lax.rem(which, 3) == 2) & (which // 3 == u)

        table = exact(selector((rows, kinds), main_of), lift_main_ref[mine], ((1,), (1,)))
        table = table + exact(selector((rows, limb_size), special_of), lift_special_ref[mine], ((1,), (1,)))
        lift_w[...] = expand(table, rows)
        rows = kinds * SUB
        table = exact(selector((rows, kinds), lambda r, t: r // SUB == t), lower_ref[...], ((1,), (1,)))
        lower_w[...] = expand(table, rows)

    ic_w[...] = weight_right(ic_ref[...])
    stage1(0)
    pl.semaphore_wait(barrier, coef_size + limb_size - 2)
    push1(0)
    build_weights()
    prepare_twist()
    for g in range(1, chunks):
        stage1(g)
        push1(g)
    push_twist()
    build_mixes()
    work = []
    for g in range(chunks):
        for k, step in enumerate((stage2, stage3, stage4, stage5, stage6, stage7, stage8, stage9)):
            work.append((k + ORDER_SKEW * g, g, k, step))
    work.sort(key=lambda w: w[:3])
    twisted = False
    for _, g, k, step in work:
        if k >= 2 and not twisted:
            build_twist()
            twisted = True
        step(g)

    for g in range(chunks):
        for stage, ref, count in (
            (0, got1, coef_size - 1), (1, got2, coef_size - 1), (2, got3, ring - 1), (3, got4, limb_size - 1),
            (4, got5, coef_size - 1), (5, got6, coef_size - 1), (6, got7, limb_size - 1), (7, got8, limb_size - 1),
        ):
            settle(ref.at[g, pl.ds(0, count)], ssem.at[stage, g])
    settle(got_t.at[pl.ds(0, coef_size - 1)], tsem.at[0])


def on_device(
    coef_size, limb_size,
    cipher_zero, cipher_one, key_main, key_special, lift_main, lift_special, lower_table, inverse_scale,
    inverse_main, inverse_special, forward_main, forward_special,
    inverse_rows, inverse_columns, forward_rows, forward_columns,
):
    ciphers = cipher_one.shape[0]
    chunks = ciphers // PART
    tile = (SUB, LANE)
    vmem = pl.BlockSpec(memory_space=pltpu.VMEM)
    smem = pl.BlockSpec(memory_space=pltpu.SMEM)
    out = jax.ShapeDtypeStruct((ciphers, 2, SUB, COLS), F32)
    item = pltpu.VMEM((chunks, coef_size) + tile, F32)
    depth = limb_size * SUB
    stages = 8
    zero, one = pl.pallas_call(
        functools.partial(kernel, coef_size, limb_size, chunks),
        out_shape=(out, out),
        in_specs=[vmem] * 7 + [smem] + [vmem] * 8,
        out_specs=(vmem, vmem),
        scratch_shapes=[
            item, item, item, item,
            pltpu.VMEM((chunks, limb_size // 2, 4) + tile, F32),
            pltpu.VMEM((chunks, limb_size, 3, 2) + tile, F32),
            pltpu.VMEM((chunks, limb_size, 3, 2) + tile, F32),
            item, item, item, item,
            pltpu.VMEM((chunks, limb_size, 2) + tile, F32),
            pltpu.VMEM((chunks, limb_size, 2, 2) + tile, F32),
            pltpu.VMEM((chunks, limb_size, 2, 2) + tile, F32),
            pltpu.VMEM((coef_size,) + tile, F32),
            pltpu.VMEM((coef_size,) + tile, F32),
            pltpu.VMEM((3, 2) + tile, F32),
            pltpu.VMEM((chunks, PART, 2, 2 * SUB, COLS), F32),
            pltpu.VMEM((3 * COLS, COLS), BF16),
            pltpu.VMEM((3 * COLS, COLS), BF16),
            pltpu.VMEM((ROWS, 3 * ROWS), BF16),
            pltpu.VMEM((3 * depth, 3 * depth), BF16),
            pltpu.VMEM((2 * depth, 3 * depth), BF16),
            pltpu.SemaphoreType.DMA((stages, chunks)),
            pltpu.SemaphoreType.DMA((stages, chunks)),
            pltpu.SemaphoreType.DMA((2,)),
        ],
        compiler_params=pltpu.CompilerParams(
            collective_id=0, has_side_effects=True, vmem_limit_bytes=40 << 20
        ),
    )(
        cipher_one.reshape(ciphers, 2, SUB, COLS),
        cipher_zero.reshape(ciphers, 2, SUB, COLS),
        key_main.reshape(ciphers, 2, 2, 2 * SUB, COLS),
        key_special.reshape(ciphers, 2, 2 * SUB, COLS),
        lift_main, lift_special, lower_table, inverse_scale,
        inverse_main, inverse_special, forward_main, forward_special,
        inverse_rows, inverse_columns, forward_rows, forward_columns,
    )
    return zero.reshape(cipher_zero.shape), one.reshape(cipher_one.shape)


def solution(mesh):
    spread = P(None, "limb", "coef")
    keys = P(None, None, None, "limb", "coef")
    local = P("limb", "coef", None)
    placed = (spread, spread, keys, keys, P(), P(), P(), P("limb"), local, local, local, local, P(), P(), P(), P())
    return jax.shard_map(
        functools.partial(on_device, mesh.shape["coef"], mesh.shape["limb"]),
        mesh=mesh,
        in_specs=placed,
        out_specs=(spread, spread),
        check_vma=False,
    )
```

```python
import functools

import jax
import jax.numpy as jnp
from jax import lax
from jax.experimental import pallas as pl
from jax.experimental.pallas import tpu as pltpu
from jax.sharding import PartitionSpec as P

F32, BF16 = jnp.float32, jnp.bfloat16
HIGHEST = lax.Precision.HIGHEST
MESH = pl.DeviceIdType.MESH
ROWS = COLS = 256
SUB, LANE = 8, 128
PART = 8
ORDER_SKEW = 0.0
SMALL = ("lift_main", "lift_special", "lower", "scale", "tim", "tis", "tfm", "tfs", "ir", "ic", "fr", "fc")


def halves(v):
    high = v.astype(BF16)
    return high, (v - high.astype(F32)).astype(BF16)


def iota(shape, axis):
    return lax.broadcasted_iota(jnp.int32, shape, axis)


def selector(shape, condition):
    return jnp.where(condition(iota(shape, 0), iota(shape, 1)), 1.0, 0.0).astype(F32)


def exact(a, b, dims):
    return lax.dot_general(a, b, (dims, ((), ())), precision=HIGHEST, preferred_element_type=F32)


def fold(a, b):
    return jnp.dot(a, b, preferred_element_type=F32)


def data_rows(v):
    high, low = halves(v)
    return jnp.concatenate([high, high, low], axis=1)


def data_columns(v):
    high, low = halves(v)
    return jnp.concatenate([high, high, low], axis=0)


def weight_right(v):
    high, low = halves(v)
    return jnp.concatenate([high, low, high], axis=0)


def weight_left(v):
    high, low = halves(v)
    return jnp.concatenate([high, low, high], axis=1)


def kernel(
    coef_size, limb_size, chunks,
    x_ref, zero_ref, km_ref, ks_ref, *rest,
):
    names = len(SMALL)
    sources, (out0_ref, out1_ref) = rest[:names], rest[names:names + 2]
    held, rest = rest[names + 2:2 * names + 2], rest[2 * names + 2:]
    lsem, rest = rest[0], rest[1:]
    loads = {
        name: pltpu.make_async_copy(source, target, lsem.at[n])
        for n, (name, source, target) in enumerate(zip(SMALL, sources, held))
    }
    for name in SMALL:
        loads[name].start()
    (lift_main_ref, lift_special_ref, lower_ref, scale_ref, tim_ref, tis_ref, tfm_ref, tfs_ref,
     ir_ref, ic_ref, fr_ref, fc_ref) = held
    body(coef_size, limb_size, chunks, loads, x_ref, zero_ref, km_ref, ks_ref,
         lift_main_ref, lift_special_ref, lower_ref, scale_ref, tim_ref, tis_ref, tfm_ref, tfs_ref,
         ir_ref, ic_ref, fr_ref, fc_ref, out0_ref, out1_ref, *rest)


def body(
    coef_size, limb_size, chunks, loads,
    x_ref, zero_ref, km_ref, ks_ref, lift_main_ref, lift_special_ref, lower_ref, scale_ref,
    tim_ref, tis_ref, tfm_ref, tfs_ref, ir_ref, ic_ref, fr_ref, fc_ref,
    out0_ref, out1_ref,
    send1, got1, send2, got3, send4, got4, send5, got5, send6, got7, send8, got8,
    send_t, got_t, twist, total, ic_w, fc_w, m_w, lift_w, lower_w,
    ssem, rsem, tsem,
):
    coef = lax.axis_index("coef")
    limb = lax.axis_index("limb")
    ring = limb_size // 2
    side = limb // ring
    place = lax.rem(limb, ring)
    core = lax.rem(coef, 2)
    chip = coef // 2
    tall = coef_size // 4
    height = lax.rem(chip, tall)

    barrier = pltpu.get_barrier_semaphore()

    @pl.loop(1, coef_size)
    def _(j):
        pl.semaphore_signal(barrier, inc=1, device_id={"coef": lax.rem(coef + j, coef_size)}, device_id_type=MESH)

    @pl.loop(1, limb_size)
    def _(j):
        pl.semaphore_signal(barrier, inc=1, device_id={"limb": lax.rem(limb + j, limb_size)}, device_id_type=MESH)

    def need(*which):
        for name in which:
            loads[name].wait()

    def push(source, target, peer, stage, g):
        pltpu.make_async_remote_copy(
            src_ref=source, dst_ref=target, send_sem=ssem.at[stage, g], recv_sem=rsem.at[stage, g],
            device_id=peer, device_id_type=MESH,
        ).start()

    def settle(ref, sem):
        pltpu.make_async_copy(ref, ref, sem).wait()

    def settle_back(got, sem, selfish):
        @pl.when(selfish)
        def _():
            settle(got.at[pl.ds(0, coef_size - 1)], sem)

        @pl.when(jnp.logical_not(selfish))
        def _():
            settle(got, sem)

    def coef_push(send, got, stage, g):
        @pl.loop(1, coef_size)
        def _(j):
            peer = lax.rem(coef + j, coef_size)
            push(send.at[g, peer], got.at[g, coef], {"coef": peer}, stage, g)

        got[g, coef] = send[g, coef]

    def coef_wait(got, stage, g):
        settle(got.at[g, pl.ds(0, coef_size - 1)], rsem.at[stage, g])

    def stage1(g):
        v = x_ref[pl.ds(PART * g, PART)].reshape(PART * 2 * SUB, COLS)
        a = fold(data_rows(v), ic_w[...]).reshape(PART, 2, SUB, COLS) * tim_ref[...][None]
        for b in range(PART):
            for h in range(2):
                for l in range(2):
                    send1[g, 4 * b + 2 * h + l] = a[b, l, :, h * LANE:(h + 1) * LANE]

    def push1(g):
        coef_push(send1, got1, 0, g)

    def rows_of(high, low):
        return high * tall + lax.rem(low + height, tall)

    def stage2(g):
        coef_wait(got1, 0, g)
        v = got1[g].reshape(ROWS, LANE)
        send2[g] = fold(m_w[...], data_columns(v)).reshape(coef_size, SUB, LANE)
        slot = 2 * place + core

        @pl.loop(1, limb_size)
        def _(j):
            to = lax.rem(slot + j, limb_size)
            low, high = to // 2, lax.rem(to, 2)
            push(
                send2.at[g, pl.ds(2 * rows_of(high, low), 2)], got3.at[g, slot],
                {"limb": side * ring + low, "coef": 2 * chip + high}, 1, g,
            )

        got3[g, slot] = send2[g, pl.ds(2 * rows_of(core, place), 2)]

    def mix_and_push(weight, got, wait_stage, send, back, stage, per, block, source, g):
        settle(got.at[g, pl.ds(0, limb_size - 1)], rsem.at[wait_stage, g])
        v = got[g]
        both = jnp.concatenate([v[:, u].reshape(limb_size * SUB, LANE) for u in range(2)], axis=1)
        w = fold(weight[...], data_columns(both)).reshape(limb_size, per, SUB, 2 * LANE)
        for u in range(2):
            send[g, :, u] = w[..., u * LANE:(u + 1) * LANE]

        @pl.loop(0, 2 * limb_size)
        def _(j):
            to = lax.rem(limb + j // 2, limb_size)
            u = lax.rem(core + j, 2)
            peer = 2 * block + u

            @pl.when((to != limb) | (peer != coef))
            def _():
                push(send.at[g, to, u], back.at[g, source], {"limb": to, "coef": peer}, stage, g)

        @pl.when(block == chip)
        def _():
            back[g, source] = send[g, limb, core]

    lift_block, lower_block = rows_of(core, place), rows_of(side, place)

    def stage3(g):
        mix_and_push(lift_w, got3, 1, send4, got4, 2, 3, lift_block, side * (coef_size // 2) + chip, g)

    def finish(v, kinds):
        n = v.shape[0]
        parts = [(v[:, h] * twist[:kinds, h][None]).reshape(n * kinds * SUB, LANE) for h in range(2)]
        rows = jnp.concatenate(parts, axis=1)
        return fold(data_rows(rows), fc_w[...]).reshape(n, kinds * SUB, COLS)

    def stage4(g):
        settle_back(got4.at[g], rsem.at[2, g], lift_block == chip)
        values = finish(got4[g].reshape(2 * PART, 2, 3, SUB, LANE), 3).reshape(2, PART, 3 * SUB, COLS)
        here = pl.ds(PART * g, PART)
        special = 0.0
        for d in range(2):
            v = values[d, :, 2 * SUB:]
            special = special + jnp.concatenate([v, v], axis=1) * ks_ref[here, d].astype(F32)
        a = fold(data_rows(special.reshape(PART * 2 * SUB, COLS)), ic_w[...])
        a = a.reshape(PART * 2, SUB, COLS) * tis_ref[...]
        for n in range(PART * 2):
            for h in range(2):
                send5[g, 2 * n + h] = a[n, :, h * LANE:(h + 1) * LANE]
        coef_push(send5, got5, 3, g)
        for i in range(2):
            total[g, :, i] = sum(
                values[d, :, :2 * SUB] * km_ref[here, d, i].astype(F32) for d in range(2)
            )

    def stage5(g):
        coef_wait(got5, 3, g)
        v = got5[g].reshape(ROWS, LANE)
        send6[g] = fold(m_w[...], data_columns(v)).reshape(coef_size, SUB, LANE)

        @pl.loop(1, limb_size)
        def _(j):
            to = lax.rem(limb + j, limb_size)
            rows = rows_of(to // ring, lax.rem(to, ring))
            push(send6.at[g, pl.ds(2 * rows, 2)], got7.at[g, limb], {"limb": to}, 4, g)

        got7[g, limb] = send6[g, pl.ds(2 * lower_block, 2)]

    def stage6(g):
        mix_and_push(lower_w, got7, 4, send8, got8, 5, 2, lower_block, coef, g)

    def stage7(g):
        settle_back(got8.at[g], rsem.at[5, g], lower_block == chip)
        low = finish(got8[g].reshape(2 * PART, 2, 2, SUB, LANE), 2).reshape(PART, 2, 2, SUB, COLS)
        here = pl.ds(PART * g, PART)
        for t in range(2):
            for i, out in enumerate((out0_ref, out1_ref)):
                result = scale_ref[t] * (total[g, :, i, t * SUB:(t + 1) * SUB] - low[:, i, t])
                out[here, t] = zero_ref[here, t] + result if i == 0 else result

    def prepare_twist():
        rows = jnp.concatenate(
            [tfm_ref[...].reshape(2 * SUB, ROWS), tfs_ref[...].reshape(SUB, ROWS), jnp.zeros((LANE - 3 * SUB, ROWS), F32)],
            axis=0,
        )
        send_t[...] = rows.T.reshape(coef_size, SUB, LANE)

    def push_twist():
        @pl.loop(1, coef_size)
        def _(j):
            peer = lax.rem(coef + j, coef_size)
            pltpu.make_async_remote_copy(
                src_ref=send_t.at[peer], dst_ref=got_t.at[coef], send_sem=tsem.at[0], recv_sem=tsem.at[1],
                device_id={"coef": peer}, device_id_type=MESH,
            ).start()

        got_t[coef] = send_t[coef]

    def build_twist():
        settle(got_t.at[pl.ds(0, coef_size - 1)], tsem.at[1])
        lanes = iota((SUB, LANE), 1) // SUB
        per = LANE // SUB
        for t in range(3):
            for h in range(2):
                value = jnp.zeros((SUB, LANE), F32)
                for q in range(per):
                    tile = got_t[h * per + q]
                    shift = (q - t) * SUB % LANE
                    moved = pltpu.roll(tile, shift, 1) if shift else tile
                    value = jnp.where(lanes == q, moved, value)
                twist[t, h] = value

    def build_weights():
        m_w[...] = weight_left(exact(fr_ref[...], ir_ref[...], ((0,), (1,))))
        fc_w[...] = weight_right(fc_ref[...])

    def build_mixes():
        depth = limb_size * SUB
        kinds = limb_size * 2

        def expand(table, spread):
            rows = table.shape[0]
            wide = exact(table, spread, ((1,), (0,)))
            keep = lax.rem(iota((rows, depth), 0), SUB) == lax.rem(iota((rows, depth), 1), SUB)
            return weight_left(jnp.where(keep, wide, 0.0))

        def main_of(r, t):
            which = r // SUB
            return (lax.rem(which, 3) < 2) & (2 * (which // 3) + lax.rem(which, 3) == t)

        def special_of(r, u):
            which = r // SUB
            return (lax.rem(which, 3) == 2) & (which // 3 == u)

        rows = limb_size * 3 * SUB
        table = exact(selector((rows, kinds), main_of), lift_main_ref[...], ((1,), (1,)))
        table = table + exact(selector((rows, limb_size), special_of), lift_special_ref[...], ((1,), (0,)))
        lift_w[...] = expand(table, selector((kinds, depth), lambda s, c: c // SUB + side * limb_size == s))
        table = exact(selector((kinds * SUB, kinds), lambda r, t: r // SUB == t), lower_ref[...], ((1,), (1,)))
        lower_w[...] = expand(table, selector((limb_size, depth), lambda s, c: c // SUB == s))

    need("ic", "tim")
    ic_w[...] = weight_right(ic_ref[...])
    stage1(0)
    pl.semaphore_wait(barrier, coef_size + limb_size - 2)
    push1(0)
    need("ir", "fr", "fc", "tfm", "tfs", "tis", "scale")
    build_weights()
    prepare_twist()
    for g in range(1, chunks):
        stage1(g)
        push1(g)
    push_twist()
    need("lift_main", "lift_special", "lower")
    build_mixes()
    work = []
    for g in range(chunks):
        for k, step in enumerate((stage2, stage3, stage4, stage5, stage6, stage7)):
            work.append((k + ORDER_SKEW * g, g, k, step))
    work.sort(key=lambda w: w[:3])
    twisted = False
    for _, g, k, step in work:
        if k >= 2 and not twisted:
            build_twist()
            twisted = True
        step(g)

    for g in range(chunks):
        for stage, ref, count in ((0, got1, coef_size - 1), (1, got3, limb_size - 1), (3, got5, coef_size - 1), (4, got7, limb_size - 1)):
            settle(ref.at[g, pl.ds(0, count)], ssem.at[stage, g])
        settle_back(got4.at[g], ssem.at[2, g], lift_block == chip)
        settle_back(got8.at[g], ssem.at[5, g], lower_block == chip)
    settle(got_t.at[pl.ds(0, coef_size - 1)], tsem.at[0])


def on_device(
    coef_size, limb_size,
    cipher_zero, cipher_one, key_main, key_special, lift_main, lift_special, lower_table, inverse_scale,
    inverse_main, inverse_special, forward_main, forward_special,
    inverse_rows, inverse_columns, forward_rows, forward_columns,
):
    ciphers = cipher_one.shape[0]
    chunks = ciphers // PART
    tile = (SUB, LANE)
    vmem = pl.BlockSpec(memory_space=pltpu.VMEM)
    small = (
        lift_main, lift_special.T, lower_table, inverse_scale, inverse_main, inverse_special, forward_main, forward_special,
        inverse_rows, inverse_columns, forward_rows, forward_columns,
    )
    out = jax.ShapeDtypeStruct((ciphers, 2, SUB, COLS), F32)
    item = pltpu.VMEM((chunks, coef_size) + tile, F32)
    depth = limb_size * SUB
    stages = 6
    zero, one = pl.pallas_call(
        functools.partial(kernel, coef_size, limb_size, chunks),
        out_shape=(out, out),
        in_specs=[vmem] * 4 + [pl.BlockSpec(memory_space=pltpu.HBM)] * len(small),
        out_specs=(vmem, vmem),
        scratch_shapes=[
            *(pltpu.SMEM(v.shape, F32) if v.ndim == 1 else pltpu.VMEM(v.shape, F32) for v in small),
            pltpu.SemaphoreType.DMA((len(small),)),
            item, item, item,
            pltpu.VMEM((chunks, limb_size, 2) + tile, F32),
            pltpu.VMEM((chunks, limb_size, 2, 3) + tile, F32),
            pltpu.VMEM((chunks, coef_size, 3) + tile, F32),
            item, item, item,
            pltpu.VMEM((chunks, limb_size, 2) + tile, F32),
            pltpu.VMEM((chunks, limb_size, 2, 2) + tile, F32),
            pltpu.VMEM((chunks, coef_size, 2) + tile, F32),
            pltpu.VMEM((coef_size,) + tile, F32),
            pltpu.VMEM((coef_size,) + tile, F32),
            pltpu.VMEM((3, 2) + tile, F32),
            pltpu.VMEM((chunks, PART, 2, 2 * SUB, COLS), F32),
            pltpu.VMEM((3 * COLS, COLS), BF16),
            pltpu.VMEM((3 * COLS, COLS), BF16),
            pltpu.VMEM((ROWS, 3 * ROWS), BF16),
            pltpu.VMEM((3 * depth, 3 * depth), BF16),
            pltpu.VMEM((2 * depth, 3 * depth), BF16),
            pltpu.SemaphoreType.DMA((stages, chunks)),
            pltpu.SemaphoreType.DMA((stages, chunks)),
            pltpu.SemaphoreType.DMA((2,)),
        ],
        compiler_params=pltpu.CompilerParams(
            collective_id=0, has_side_effects=True, vmem_limit_bytes=40 << 20
        ),
    )(
        cipher_one.reshape(ciphers, 2, SUB, COLS),
        cipher_zero.reshape(ciphers, 2, SUB, COLS),
        key_main.reshape(ciphers, 2, 2, 2 * SUB, COLS),
        key_special.reshape(ciphers, 2, 2 * SUB, COLS),
        *(pltpu.with_memory_space_constraint(v, pltpu.HBM) for v in small),
    )
    return zero.reshape(cipher_zero.shape), one.reshape(cipher_one.shape)


def solution(mesh):
    spread = P(None, "limb", "coef")
    keys = P(None, None, None, "limb", "coef")
    local = P("limb", "coef", None)
    placed = (spread, spread, keys, keys, P(), P(), P(), P("limb"), local, local, local, local, P(), P(), P(), P())
    return jax.shard_map(
        functools.partial(on_device, mesh.shape["coef"], mesh.shape["limb"]),
        mesh=mesh,
        in_specs=placed,
        out_specs=(spread, spread),
        check_vma=False,
    )
```

```python
import functools

import jax
import jax.numpy as jnp
from jax import lax
from jax.experimental import pallas as pl
from jax.experimental.pallas import tpu as pltpu
from jax.sharding import PartitionSpec as P

F32, BF16 = jnp.float32, jnp.bfloat16
HIGHEST = lax.Precision.HIGHEST
MESH = pl.DeviceIdType.MESH
ROWS = COLS = 256
SUB, LANE = 8, 128
PART = 8
SMALL = ("lift_main", "lift_special", "lower", "scale", "tim", "tis", "tfm", "tfs", "ir", "ic", "fr", "fc")


def halves(v):
    high = v.astype(BF16)
    return high, (v - high.astype(F32)).astype(BF16)


def iota(shape, axis):
    return lax.broadcasted_iota(jnp.int32, shape, axis)


def selector(shape, condition):
    return jnp.where(condition(iota(shape, 0), iota(shape, 1)), 1.0, 0.0).astype(F32)


def exact(a, b, dims):
    return lax.dot_general(a, b, (dims, ((), ())), precision=HIGHEST, preferred_element_type=F32)


def fold(a, b):
    return jnp.dot(a, b, preferred_element_type=F32)


def data_rows(v):
    high, low = halves(v)
    return jnp.concatenate([high, high, low], axis=1)


def data_columns(v):
    high, low = halves(v)
    return jnp.concatenate([high, high, low], axis=0)


def weight_right(v):
    high, low = halves(v)
    return jnp.concatenate([high, low, high], axis=0)


def weight_left(v):
    high, low = halves(v)
    return jnp.concatenate([high, low, high], axis=1)


def kernel(
    coef_size, limb_size, chunks,
    x_ref, zero_ref, km_ref, ks_ref, *rest,
):
    names = len(SMALL)
    sources, (out0_ref, out1_ref) = rest[:names], rest[names:names + 2]
    held, rest = rest[names + 2:2 * names + 2], rest[2 * names + 2:]
    lsem, rest = rest[0], rest[1:]
    loads = {
        name: pltpu.make_async_copy(source, target, lsem.at[n])
        for n, (name, source, target) in enumerate(zip(SMALL, sources, held))
    }
    for name in SMALL:
        loads[name].start()
    (lift_main_ref, lift_special_ref, lower_ref, scale_ref, tim_ref, tis_ref, tfm_ref, tfs_ref,
     ir_ref, ic_ref, fr_ref, fc_ref) = held
    body(coef_size, limb_size, chunks, loads, x_ref, zero_ref, km_ref, ks_ref,
         lift_main_ref, lift_special_ref, lower_ref, scale_ref, tim_ref, tis_ref, tfm_ref, tfs_ref,
         ir_ref, ic_ref, fr_ref, fc_ref, out0_ref, out1_ref, *rest)


def body(
    coef_size, limb_size, chunks, loads,
    x_ref, zero_ref, km_ref, ks_ref, lift_main_ref, lift_special_ref, lower_ref, scale_ref,
    tim_ref, tis_ref, tfm_ref, tfs_ref, ir_ref, ic_ref, fr_ref, fc_ref,
    out0_ref, out1_ref,
    send1, got1, send2, got2, got3, send_s, got_s, send_m, got_m, send5, got5, send6, got6, got7, send8, got8,
    send_t, got_t, twist, total, ic_w, fc_w, m_w, special_w, main_w, lower_w,
    ssem, rsem, tsem,
):
    coef = lax.axis_index("coef")
    limb = lax.axis_index("limb")
    ring = limb_size // 2
    side = limb // ring
    place = lax.rem(limb, ring)

    barrier = pltpu.get_barrier_semaphore()

    @pl.loop(1, coef_size)
    def _(j):
        pl.semaphore_signal(barrier, inc=1, device_id={"coef": lax.rem(coef + j, coef_size)}, device_id_type=MESH)

    @pl.loop(1, limb_size)
    def _(j):
        pl.semaphore_signal(barrier, inc=1, device_id={"limb": lax.rem(limb + j, limb_size)}, device_id_type=MESH)

    def need(*which):
        for name in which:
            loads[name].wait()

    def push(source, target, axis, peer, stage, g):
        pltpu.make_async_remote_copy(
            src_ref=source, dst_ref=target, send_sem=ssem.at[stage, g], recv_sem=rsem.at[stage, g],
            device_id={axis: peer}, device_id_type=MESH,
        ).start()

    def settle(ref, sem):
        pltpu.make_async_copy(ref, ref, sem).wait()

    def coef_push(send, got, stage, g):
        @pl.loop(1, coef_size)
        def _(j):
            peer = lax.rem(coef + j, coef_size)
            push(send.at[g, peer], got.at[g, coef], "coef", peer, stage, g)

        got[g, coef] = send[g, coef]

    def coef_wait(got, stage, g):
        settle(got.at[g, pl.ds(0, coef_size - 1)], rsem.at[stage, g])

    def to_items(ref, g, v):
        for n in range(v.shape[0]):
            for h in range(2):
                ref[g, 2 * n + h] = v[n, :, h * LANE:(h + 1) * LANE]

    def stage1(g):
        v = x_ref[pl.ds(PART * g, PART)].reshape(PART * 2 * SUB, COLS)
        a = fold(data_rows(v), ic_w[...]).reshape(PART, 2, SUB, COLS) * tim_ref[...][None]
        to_items(send1, g, a.reshape(PART * 2, SUB, COLS))

    def push1(g):
        coef_push(send1, got1, 0, g)

    def stage2(g):
        coef_wait(got1, 0, g)
        v = got1[g].reshape(ROWS, LANE)
        send2[g] = fold(m_w[...], data_columns(v)).reshape(coef_size, SUB, LANE)
        coef_push(send2, got2, 1, g)

    def stage3(g):
        coef_wait(got2, 1, g)

        @pl.loop(1, ring)
        def _(j):
            to = lax.rem(place + j, ring)
            push(got2.at[g, pl.ds(4 * to, 4)], got3.at[g, place], "limb", side * ring + to, 2, g)

        got3[g, place] = got2[g, pl.ds(4 * place, 4)]

    def mixed(weight, got, send, per, g):
        v = got[g].reshape(limb_size, 2, SUB, LANE)
        both = jnp.concatenate([v[:, h].reshape(limb_size * SUB, LANE) for h in range(2)], axis=1)
        w = fold(weight[...], data_columns(both)).reshape(limb_size, per, SUB, 2 * LANE)
        for h in range(2):
            send[g, :, :, h] = w[..., h * LANE:(h + 1) * LANE]

    def limb_wait(got, stage, g, count=limb_size - 1):
        settle(got.at[g, pl.ds(0, count)], rsem.at[stage, g])

    def limb_push(send, got, stage, g):
        @pl.loop(1, limb_size)
        def _(j):
            peer = lax.rem(limb + j, limb_size)
            push(send.at[g, peer], got.at[g, limb], "limb", peer, stage, g)

        got[g, limb] = send[g, limb]

    def stage4_special(g):
        limb_wait(got3, 2, g, ring - 1)
        mixed(special_w, got3, send_s, 1, g)
        limb_push(send_s, got_s, 3, g)

    def stage4_main(g):
        mixed(main_w, got3, send_m, 2, g)
        limb_push(send_m, got_m, 8, g)

    def finish(v, scale):
        n, kinds = v.shape[:2]
        parts = [(v[:, :, h] * scale[:, h][None]).reshape(n * kinds * SUB, LANE) for h in range(2)]
        rows = jnp.concatenate(parts, axis=1)
        return fold(data_rows(rows), fc_w[...]).reshape(n, kinds * SUB, COLS)

    def stage5(g):
        limb_wait(got_s, 3, g)
        values = finish(got_s[g], twist[2:]).reshape(2, PART, SUB, COLS)
        here = pl.ds(PART * g, PART)
        special = sum(
            jnp.concatenate([values[d], values[d]], axis=1) * ks_ref[here, d].astype(F32) for d in range(2)
        )
        a = fold(data_rows(special.reshape(PART * 2 * SUB, COLS)), ic_w[...])
        a = a.reshape(PART * 2, SUB, COLS) * tis_ref[...]
        to_items(send5, g, a)
        coef_push(send5, got5, 4, g)

    def stage5_main(g):
        limb_wait(got_m, 8, g)
        values = finish(got_m[g], twist[:2]).reshape(2, PART, 2 * SUB, COLS)
        here = pl.ds(PART * g, PART)
        for i in range(2):
            total[g, :, i] = sum(values[d] * km_ref[here, d, i].astype(F32) for d in range(2))

    def stage6(g):
        coef_wait(got5, 4, g)
        v = got5[g].reshape(ROWS, LANE)
        send6[g] = fold(m_w[...], data_columns(v)).reshape(coef_size, SUB, LANE)
        coef_push(send6, got6, 5, g)

    def stage7(g):
        coef_wait(got6, 5, g)

        @pl.loop(1, limb_size)
        def _(j):
            to = lax.rem(limb + j, limb_size)
            push(got6.at[g, pl.ds(2 * to, 2)], got7.at[g, limb], "limb", to, 6, g)

        got7[g, limb] = got6[g, pl.ds(2 * limb, 2)]

    def stage8(g):
        limb_wait(got7, 6, g)
        mixed(lower_w, got7, send8, 2, g)
        limb_push(send8, got8, 7, g)

    def stage9(g):
        limb_wait(got8, 7, g)
        low = finish(got8[g], twist[:2]).reshape(PART, 2, 2, SUB, COLS)
        here = pl.ds(PART * g, PART)
        for t in range(2):
            for i, out in enumerate((out0_ref, out1_ref)):
                result = scale_ref[t] * (total[g, :, i, t * SUB:(t + 1) * SUB] - low[:, i, t])
                out[here, t] = zero_ref[here, t] + result if i == 0 else result

    def prepare_twist():
        rows = jnp.concatenate(
            [tfm_ref[...].reshape(2 * SUB, ROWS), tfs_ref[...].reshape(SUB, ROWS), jnp.zeros((LANE - 3 * SUB, ROWS), F32)],
            axis=0,
        )
        send_t[...] = rows.T.reshape(coef_size, SUB, LANE)

    def push_twist():
        @pl.loop(1, coef_size)
        def _(j):
            peer = lax.rem(coef + j, coef_size)
            pltpu.make_async_remote_copy(
                src_ref=send_t.at[peer], dst_ref=got_t.at[coef], send_sem=tsem.at[0], recv_sem=tsem.at[1],
                device_id={"coef": peer}, device_id_type=MESH,
            ).start()

        got_t[coef] = send_t[coef]

    def build_twist():
        settle(got_t.at[pl.ds(0, coef_size - 1)], tsem.at[1])
        lanes = iota((SUB, LANE), 1) // SUB
        per = LANE // SUB
        for t in range(3):
            for h in range(2):
                value = jnp.zeros((SUB, LANE), F32)
                for q in range(per):
                    tile = got_t[h * per + q]
                    shift = (q - t) * SUB % LANE
                    moved = pltpu.roll(tile, shift, 1) if shift else tile
                    value = jnp.where(lanes == q, moved, value)
                twist[t, h] = value

    def build_weights():
        m_w[...] = weight_left(exact(fr_ref[...], ir_ref[...], ((0,), (1,))))
        fc_w[...] = weight_right(fc_ref[...])

    def build_mixes():
        depth = limb_size * SUB
        kinds = limb_size * 2

        def expand(table, spread):
            rows = table.shape[0]
            wide = exact(table, spread, ((1,), (0,)))
            keep = lax.rem(iota((rows, depth), 0), SUB) == lax.rem(iota((rows, depth), 1), SUB)
            return weight_left(jnp.where(keep, wide, 0.0))

        pick = selector((kinds * SUB, kinds), lambda r, t: r // SUB == t)
        mine = selector((kinds, depth), lambda s, c: c // SUB + side * limb_size == s)
        table = exact(selector((depth, limb_size), lambda r, u: r // SUB == u), lift_special_ref[...], ((1,), (0,)))
        special_w[...] = expand(table, mine)
        main_w[...] = expand(exact(pick, lift_main_ref[...], ((1,), (1,))), mine)
        table = exact(pick, lower_ref[...], ((1,), (1,)))
        lower_w[...] = expand(table, selector((limb_size, depth), lambda s, c: c // SUB == s))

    every = range(chunks)
    need("ic", "tim")
    ic_w[...] = weight_right(ic_ref[...])
    for g in every:
        stage1(g)
    pl.semaphore_wait(barrier, coef_size + limb_size - 2)
    for g in every:
        push1(g)
    need("ir", "fr", "fc", "tfm", "tfs", "tis", "scale", "lift_main", "lift_special", "lower")
    build_weights()
    for g in every:
        stage2(g)
    prepare_twist()
    push_twist()
    build_mixes()
    for step in (stage3, stage4_special, stage4_main):
        for g in every:
            step(g)
    build_twist()
    for step in (stage5, stage6, stage7, stage8, stage5_main, stage9):
        for g in every:
            step(g)

    for g in range(chunks):
        for stage, ref, count in (
            (0, got1, coef_size - 1), (1, got2, coef_size - 1), (2, got3, ring - 1), (3, got_s, limb_size - 1), (8, got_m, limb_size - 1),
            (4, got5, coef_size - 1), (5, got6, coef_size - 1), (6, got7, limb_size - 1), (7, got8, limb_size - 1),
        ):
            settle(ref.at[g, pl.ds(0, count)], ssem.at[stage, g])
    settle(got_t.at[pl.ds(0, coef_size - 1)], tsem.at[0])


def on_device(
    coef_size, limb_size,
    cipher_zero, cipher_one, key_main, key_special, lift_main, lift_special, lower_table, inverse_scale,
    inverse_main, inverse_special, forward_main, forward_special,
    inverse_rows, inverse_columns, forward_rows, forward_columns,
):
    ciphers = cipher_one.shape[0]
    chunks = ciphers // PART
    tile = (SUB, LANE)
    vmem = pl.BlockSpec(memory_space=pltpu.VMEM)
    small = (
        lift_main, lift_special.T, lower_table, inverse_scale, inverse_main, inverse_special, forward_main, forward_special,
        inverse_rows, inverse_columns, forward_rows, forward_columns,
    )
    out = jax.ShapeDtypeStruct((ciphers, 2, SUB, COLS), F32)
    item = pltpu.VMEM((chunks, coef_size) + tile, F32)
    depth = limb_size * SUB
    stages = 9
    zero, one = pl.pallas_call(
        functools.partial(kernel, coef_size, limb_size, chunks),
        out_shape=(out, out),
        in_specs=[vmem] * 4 + [pl.BlockSpec(memory_space=pltpu.HBM)] * len(small),
        out_specs=(vmem, vmem),
        scratch_shapes=[
            *(pltpu.SMEM(v.shape, F32) if v.ndim == 1 else pltpu.VMEM(v.shape, F32) for v in small),
            pltpu.SemaphoreType.DMA((len(small),)),
            item, item, item, item,
            pltpu.VMEM((chunks, limb_size // 2, 4) + tile, F32),
            pltpu.VMEM((chunks, limb_size, 1, 2) + tile, F32),
            pltpu.VMEM((chunks, limb_size, 1, 2) + tile, F32),
            pltpu.VMEM((chunks, limb_size, 2, 2) + tile, F32),
            pltpu.VMEM((chunks, limb_size, 2, 2) + tile, F32),
            item, item, item, item,
            pltpu.VMEM((chunks, limb_size, 2) + tile, F32),
            pltpu.VMEM((chunks, limb_size, 2, 2) + tile, F32),
            pltpu.VMEM((chunks, limb_size, 2, 2) + tile, F32),
            pltpu.VMEM((coef_size,) + tile, F32),
            pltpu.VMEM((coef_size,) + tile, F32),
            pltpu.VMEM((3, 2) + tile, F32),
            pltpu.VMEM((chunks, PART, 2, 2 * SUB, COLS), F32),
            pltpu.VMEM((3 * COLS, COLS), BF16),
            pltpu.VMEM((3 * COLS, COLS), BF16),
            pltpu.VMEM((ROWS, 3 * ROWS), BF16),
            pltpu.VMEM((depth, 3 * depth), BF16),
            pltpu.VMEM((2 * depth, 3 * depth), BF16),
            pltpu.VMEM((2 * depth, 3 * depth), BF16),
            pltpu.SemaphoreType.DMA((stages, chunks)),
            pltpu.SemaphoreType.DMA((stages, chunks)),
            pltpu.SemaphoreType.DMA((2,)),
        ],
        compiler_params=pltpu.CompilerParams(
            collective_id=0, has_side_effects=True, vmem_limit_bytes=40 << 20
        ),
    )(
        cipher_one.reshape(ciphers, 2, SUB, COLS),
        cipher_zero.reshape(ciphers, 2, SUB, COLS),
        key_main.reshape(ciphers, 2, 2, 2 * SUB, COLS),
        key_special.reshape(ciphers, 2, 2 * SUB, COLS),
        *(pltpu.with_memory_space_constraint(v, pltpu.HBM) for v in small),
    )
    return zero.reshape(cipher_zero.shape), one.reshape(cipher_one.shape)


def solution(mesh):
    spread = P(None, "limb", "coef")
    keys = P(None, None, None, "limb", "coef")
    local = P("limb", "coef", None)
    placed = (spread, spread, keys, keys, P(), P(), P(), P("limb"), local, local, local, local, P(), P(), P(), P())
    return jax.shard_map(
        functools.partial(on_device, mesh.shape["coef"], mesh.shape["limb"]),
        mesh=mesh,
        in_specs=placed,
        out_specs=(spread, spread),
        check_vma=False,
    )
```

```python
import functools

import jax
import jax.numpy as jnp
from jax import lax
from jax.experimental import pallas as pl
from jax.experimental.pallas import tpu as pltpu
from jax.sharding import PartitionSpec as P

F32, BF16 = jnp.float32, jnp.bfloat16
HIGHEST = lax.Precision.HIGHEST
MESH = pl.DeviceIdType.MESH
ROWS = COLS = 256
SUB, LANE = 8, 128
PART = 8
SMALL = ("lift_main", "lift_special", "lower", "scale", "tim", "tis", "tfm", "tfs", "ir", "ic", "fr", "fc")


def halves(v):
    high = v.astype(BF16)
    return high, (v - high.astype(F32)).astype(BF16)


def iota(shape, axis):
    return lax.broadcasted_iota(jnp.int32, shape, axis)


def selector(shape, condition):
    return jnp.where(condition(iota(shape, 0), iota(shape, 1)), 1.0, 0.0).astype(F32)


def exact(a, b, dims):
    return lax.dot_general(a, b, (dims, ((), ())), precision=HIGHEST, preferred_element_type=F32)


def fold(a, b):
    return jnp.dot(a, b, preferred_element_type=F32)


def data_rows(v):
    high, low = halves(v)
    return jnp.concatenate([high, high, low], axis=1)


def data_columns(v):
    high, low = halves(v)
    return jnp.concatenate([high, high, low], axis=0)


def weight_right(v):
    high, low = halves(v)
    return jnp.concatenate([high, low, high], axis=0)


def weight_left(v):
    high, low = halves(v)
    return jnp.concatenate([high, low, high], axis=1)


def kernel(
    coef_size, limb_size, chunks,
    x_ref, km_ref, ks_ref, *rest,
):
    names = len(SMALL)
    sources, (out0_ref, out1_ref) = rest[:names], rest[names:names + 2]
    held, rest = rest[names + 2:2 * names + 2], rest[2 * names + 2:]
    lsem, rest = rest[0], rest[1:]
    loads = {
        name: pltpu.make_async_copy(source, target, lsem.at[n])
        for n, (name, source, target) in enumerate(zip(SMALL, sources, held))
    }
    for name in ("ic", "tim") + tuple(n for n in SMALL if n not in ("ic", "tim")):
        loads[name].start()
    (lift_main_ref, lift_special_ref, lower_ref, scale_ref, tim_ref, tis_ref, tfm_ref, tfs_ref,
     ir_ref, ic_ref, fr_ref, fc_ref) = held
    body(coef_size, limb_size, chunks, loads, x_ref, km_ref, ks_ref,
         lift_main_ref, lift_special_ref, lower_ref, scale_ref, tim_ref, tis_ref, tfm_ref, tfs_ref,
         ir_ref, ic_ref, fr_ref, fc_ref, out0_ref, out1_ref, *rest)


def body(
    coef_size, limb_size, chunks, loads,
    x_ref, km_ref, ks_ref, lift_main_ref, lift_special_ref, lower_ref, scale_ref,
    tim_ref, tis_ref, tfm_ref, tfs_ref, ir_ref, ic_ref, fr_ref, fc_ref,
    out0_ref, out1_ref,
    send1, got1, send2, got2, got3, send_s, got_s, send_m, got_m, send5, got5, send6, got6, got7, send8, got8,
    send_t, got_t, twist, total, ic_w, fc_w, m_w, special_w, main_w, lower_w,
    ssem, rsem, tsem,
):
    coef = lax.axis_index("coef")
    limb = lax.axis_index("limb")
    ring = limb_size // 2
    side = limb // ring
    place = lax.rem(limb, ring)

    barrier = pltpu.get_barrier_semaphore()

    @pl.loop(1, coef_size)
    def _(j):
        pl.semaphore_signal(barrier, inc=1, device_id={"coef": lax.rem(coef + j, coef_size)}, device_id_type=MESH)

    @pl.loop(1, limb_size)
    def _(j):
        pl.semaphore_signal(barrier, inc=1, device_id={"limb": lax.rem(limb + j, limb_size)}, device_id_type=MESH)

    def need(*which):
        for name in which:
            loads[name].wait()

    def push(source, target, axis, peer, stage, g):
        pltpu.make_async_remote_copy(
            src_ref=source, dst_ref=target, send_sem=ssem.at[stage, g], recv_sem=rsem.at[stage, g],
            device_id={axis: peer}, device_id_type=MESH,
        ).start()

    def settle(ref, sem):
        pltpu.make_async_copy(ref, ref, sem).wait()

    tall = coef_size // 4
    chip = coef // 2

    def far_first(j):
        m = j // 4
        odd = lax.rem(m, 2)
        up = odd * (tall // 2 - 1 - m // 2) + (1 - odd) * (tall // 2 + m // 2)
        across = lax.rem(chip // tall + 1 - lax.rem(j // 2, 2), 2)
        return (across * tall + lax.rem(lax.rem(chip, tall) + up, tall)) * 2 + lax.rem(coef + 1 - lax.rem(j, 2), 2)

    def coef_push(send, got, stage, g):
        @pl.loop(0, coef_size - 1)
        def _(j):
            peer = far_first(j)
            push(send.at[g, peer], got.at[g, coef], "coef", peer, stage, g)

        got[g, coef] = send[g, coef]

    def coef_wait(got, stage, g):
        settle(got.at[g, pl.ds(0, coef_size - 1)], rsem.at[stage, g])

    def to_items(ref, g, v):
        for n in range(v.shape[0]):
            for h in range(2):
                ref[g, 2 * n + h] = v[n, :, h * LANE:(h + 1) * LANE]

    def stage1(g):
        v = x_ref[pl.ds(PART * g, PART)].reshape(PART * 2 * SUB, COLS)
        a = fold(data_rows(v), ic_w[...]).reshape(PART, 2, SUB, COLS) * tim_ref[...][None]
        to_items(send1, g, a.reshape(PART * 2, SUB, COLS))

    def push1(g):
        coef_push(send1, got1, 0, g)

    def stage2(g):
        coef_wait(got1, 0, g)
        v = got1[g].reshape(ROWS, LANE)
        send2[g] = fold(m_w[...], data_columns(v)).reshape(coef_size, SUB, LANE)
        coef_push(send2, got2, 1, g)

    def stage3(g):
        coef_wait(got2, 1, g)

        @pl.loop(1, ring)
        def _(j):
            to = lax.rem(place + j, ring)
            push(got2.at[g, pl.ds(4 * to, 4)], got3.at[g, place], "limb", side * ring + to, 2, g)

        got3[g, place] = got2[g, pl.ds(4 * place, 4)]

    def mixed(weight, got, send, per, g):
        v = got[g].reshape(limb_size, 2, SUB, LANE)
        both = jnp.concatenate([v[:, h].reshape(limb_size * SUB, LANE) for h in range(2)], axis=1)
        w = fold(weight[...], data_columns(both)).reshape(limb_size, per, SUB, 2 * LANE)
        for h in range(2):
            send[g, :, :, h] = w[..., h * LANE:(h + 1) * LANE]

    def limb_wait(got, stage, g, count=limb_size - 1):
        settle(got.at[g, pl.ds(0, count)], rsem.at[stage, g])

    def limb_push(send, got, stage, g):
        @pl.loop(1, limb_size)
        def _(j):
            peer = lax.rem(limb + j, limb_size)
            push(send.at[g, peer], got.at[g, limb], "limb", peer, stage, g)

        got[g, limb] = send[g, limb]

    def stage4_special(g):
        limb_wait(got3, 2, g, ring - 1)
        mixed(special_w, got3, send_s, 1, g)
        limb_push(send_s, got_s, 3, g)

    def stage4_main(g):
        mixed(main_w, got3, send_m, 2, g)
        limb_push(send_m, got_m, 8, g)

    def finish(v, scale):
        n, kinds = v.shape[:2]
        parts = [(v[:, :, h] * scale[:, h][None]).reshape(n * kinds * SUB, LANE) for h in range(2)]
        rows = jnp.concatenate(parts, axis=1)
        return fold(data_rows(rows), fc_w[...]).reshape(n, kinds * SUB, COLS)

    def stage5(g):
        limb_wait(got_s, 3, g)
        values = finish(got_s[g], twist[2:]).reshape(2, PART, SUB, COLS)
        here = pl.ds(PART * g, PART)
        special = sum(
            jnp.concatenate([values[d], values[d]], axis=1) * ks_ref[here, d].astype(F32) for d in range(2)
        )
        a = fold(data_rows(special.reshape(PART * 2 * SUB, COLS)), ic_w[...])
        a = a.reshape(PART * 2, SUB, COLS) * tis_ref[...]
        to_items(send5, g, a)
        coef_push(send5, got5, 4, g)

    def stage5_main(g):
        limb_wait(got_m, 8, g)
        values = finish(got_m[g], twist[:2]).reshape(2, PART, 2 * SUB, COLS)
        here = pl.ds(PART * g, PART)
        for i in range(2):
            total[g, :, i] = sum(values[d] * km_ref[here, d, i].astype(F32) for d in range(2))

    def stage6(g):
        coef_wait(got5, 4, g)
        v = got5[g].reshape(ROWS, LANE)
        send6[g] = fold(m_w[...], data_columns(v)).reshape(coef_size, SUB, LANE)
        coef_push(send6, got6, 5, g)

    def stage7(g):
        coef_wait(got6, 5, g)

        @pl.loop(1, limb_size)
        def _(j):
            to = lax.rem(limb + j, limb_size)
            push(got6.at[g, pl.ds(2 * to, 2)], got7.at[g, limb], "limb", to, 6, g)

        got7[g, limb] = got6[g, pl.ds(2 * limb, 2)]

    def stage8(g):
        limb_wait(got7, 6, g)
        mixed(lower_w, got7, send8, 2, g)
        limb_push(send8, got8, 7, g)

    def stage9(g):
        limb_wait(got8, 7, g)
        low = finish(got8[g], twist[:2]).reshape(PART, 2, 2, SUB, COLS)
        here = pl.ds(PART * g, PART)
        for t in range(2):
            for i, out in enumerate((out0_ref, out1_ref)):
                out[here, t] = scale_ref[t] * (total[g, :, i, t * SUB:(t + 1) * SUB] - low[:, i, t])

    def prepare_twist():
        rows = jnp.concatenate(
            [tfm_ref[...].reshape(2 * SUB, ROWS), tfs_ref[...].reshape(SUB, ROWS), jnp.zeros((LANE - 3 * SUB, ROWS), F32)],
            axis=0,
        )
        send_t[...] = rows.T.reshape(coef_size, SUB, LANE)

    def push_twist():
        @pl.loop(1, coef_size)
        def _(j):
            peer = lax.rem(coef + j, coef_size)
            pltpu.make_async_remote_copy(
                src_ref=send_t.at[peer], dst_ref=got_t.at[coef], send_sem=tsem.at[0], recv_sem=tsem.at[1],
                device_id={"coef": peer}, device_id_type=MESH,
            ).start()

        got_t[coef] = send_t[coef]

    def build_twist():
        settle(got_t.at[pl.ds(0, coef_size - 1)], tsem.at[1])
        lanes = iota((SUB, LANE), 1) // SUB
        per = LANE // SUB
        for t in range(3):
            for h in range(2):
                value = jnp.zeros((SUB, LANE), F32)
                for q in range(per):
                    tile = got_t[h * per + q]
                    shift = (q - t) * SUB % LANE
                    moved = pltpu.roll(tile, shift, 1) if shift else tile
                    value = jnp.where(lanes == q, moved, value)
                twist[t, h] = value

    def build_weights():
        m_w[...] = weight_left(exact(fr_ref[...], ir_ref[...], ((0,), (1,))))
        fc_w[...] = weight_right(fc_ref[...])

    def build_mixes():
        depth = limb_size * SUB
        kinds = limb_size * 2

        def expand(table, spread):
            rows = table.shape[0]
            wide = exact(table, spread, ((1,), (0,)))
            keep = lax.rem(iota((rows, depth), 0), SUB) == lax.rem(iota((rows, depth), 1), SUB)
            return weight_left(jnp.where(keep, wide, 0.0))

        pick = selector((kinds * SUB, kinds), lambda r, t: r // SUB == t)
        mine = selector((kinds, depth), lambda s, c: c // SUB + side * limb_size == s)
        table = exact(selector((depth, limb_size), lambda r, u: r // SUB == u), lift_special_ref[...], ((1,), (0,)))
        special_w[...] = expand(table, mine)
        main_w[...] = expand(exact(pick, lift_main_ref[...], ((1,), (1,))), mine)
        table = exact(pick, lower_ref[...], ((1,), (1,)))
        lower_w[...] = expand(table, selector((limb_size, depth), lambda s, c: c // SUB == s))

    every = range(chunks)
    need("ic", "tim")
    ic_w[...] = weight_right(ic_ref[...])
    for g in every:
        stage1(g)
    pl.semaphore_wait(barrier, coef_size + limb_size - 2)
    for g in every:
        push1(g)
    need("ir", "fr", "fc", "tfm", "tfs", "tis", "scale", "lift_main", "lift_special", "lower")
    build_weights()
    build_mixes()
    prepare_twist()
    for g in every:
        stage2(g)
    for g in every:
        stage3(g)
    push_twist()
    for step in (stage4_special, stage4_main):
        for g in every:
            step(g)
    build_twist()
    for step in (stage5, stage6, stage7, stage8, stage5_main, stage9):
        for g in every:
            step(g)

    for g in range(chunks):
        for stage, ref, count in (
            (0, got1, coef_size - 1), (1, got2, coef_size - 1), (2, got3, ring - 1), (3, got_s, limb_size - 1), (8, got_m, limb_size - 1),
            (4, got5, coef_size - 1), (5, got6, coef_size - 1), (6, got7, limb_size - 1), (7, got8, limb_size - 1),
        ):
            settle(ref.at[g, pl.ds(0, count)], ssem.at[stage, g])
    settle(got_t.at[pl.ds(0, coef_size - 1)], tsem.at[0])


def on_device(
    coef_size, limb_size,
    cipher_zero, cipher_one, key_main, key_special, lift_main, lift_special, lower_table, inverse_scale,
    inverse_main, inverse_special, forward_main, forward_special,
    inverse_rows, inverse_columns, forward_rows, forward_columns,
):
    ciphers = cipher_one.shape[0]
    chunks = ciphers // PART
    tile = (SUB, LANE)
    vmem = pl.BlockSpec(memory_space=pltpu.VMEM)
    small = (
        lift_main, lift_special.T, lower_table, inverse_scale, inverse_main, inverse_special, forward_main, forward_special,
        inverse_rows, inverse_columns, forward_rows, forward_columns,
    )
    out = jax.ShapeDtypeStruct((ciphers, 2, SUB, COLS), F32)
    item = pltpu.VMEM((chunks, coef_size) + tile, F32)
    depth = limb_size * SUB
    stages = 9
    zero, one = pl.pallas_call(
        functools.partial(kernel, coef_size, limb_size, chunks),
        out_shape=(out, out),
        in_specs=[vmem] * 3 + [pl.BlockSpec(memory_space=pltpu.HBM)] * len(small),
        out_specs=(vmem, vmem),
        scratch_shapes=[
            *(pltpu.SMEM(v.shape, F32) if v.ndim == 1 else pltpu.VMEM(v.shape, F32) for v in small),
            pltpu.SemaphoreType.DMA((len(small),)),
            item, item, item, item,
            pltpu.VMEM((chunks, limb_size // 2, 4) + tile, F32),
            pltpu.VMEM((chunks, limb_size, 1, 2) + tile, F32),
            pltpu.VMEM((chunks, limb_size, 1, 2) + tile, F32),
            pltpu.VMEM((chunks, limb_size, 2, 2) + tile, F32),
            pltpu.VMEM((chunks, limb_size, 2, 2) + tile, F32),
            item, item, item, item,
            pltpu.VMEM((chunks, limb_size, 2) + tile, F32),
            pltpu.VMEM((chunks, limb_size, 2, 2) + tile, F32),
            pltpu.VMEM((chunks, limb_size, 2, 2) + tile, F32),
            pltpu.VMEM((coef_size,) + tile, F32),
            pltpu.VMEM((coef_size,) + tile, F32),
            pltpu.VMEM((3, 2) + tile, F32),
            pltpu.VMEM((chunks, PART, 2, 2 * SUB, COLS), F32),
            pltpu.VMEM((3 * COLS, COLS), BF16),
            pltpu.VMEM((3 * COLS, COLS), BF16),
            pltpu.VMEM((ROWS, 3 * ROWS), BF16),
            pltpu.VMEM((depth, 3 * depth), BF16),
            pltpu.VMEM((2 * depth, 3 * depth), BF16),
            pltpu.VMEM((2 * depth, 3 * depth), BF16),
            pltpu.SemaphoreType.DMA((stages, chunks)),
            pltpu.SemaphoreType.DMA((stages, chunks)),
            pltpu.SemaphoreType.DMA((2,)),
        ],
        compiler_params=pltpu.CompilerParams(
            collective_id=0, has_side_effects=True, vmem_limit_bytes=40 << 20
        ),
    )(
        cipher_one.reshape(ciphers, 2, SUB, COLS),
        key_main.reshape(ciphers, 2, 2, 2 * SUB, COLS),
        key_special.reshape(ciphers, 2, 2 * SUB, COLS),
        *(pltpu.with_memory_space_constraint(v, pltpu.HBM) for v in small),
    )
    return cipher_zero + zero.reshape(cipher_zero.shape), one.reshape(cipher_one.shape)


def solution(mesh):
    spread = P(None, "limb", "coef")
    keys = P(None, None, None, "limb", "coef")
    local = P("limb", "coef", None)
    placed = (spread, spread, keys, keys, P(), P(), P(), P("limb"), local, local, local, local, P(), P(), P(), P())
    return jax.shard_map(
        functools.partial(on_device, mesh.shape["coef"], mesh.shape["limb"]),
        mesh=mesh,
        in_specs=placed,
        out_specs=(spread, spread),
        check_vma=False,
    )
```

```python
import functools

import jax
import jax.numpy as jnp
from jax import lax
from jax.experimental import pallas as pl
from jax.experimental.pallas import tpu as pltpu
from jax.sharding import PartitionSpec as P

F32, BF16 = jnp.float32, jnp.bfloat16
HIGHEST = lax.Precision.HIGHEST
MESH = pl.DeviceIdType.MESH
ROWS = COLS = 256
SUB, LANE = 8, 128
PART = 8
SMALL = ("lift_main", "lift_special", "lower", "scale", "tim", "tis", "tfm", "tfs", "ir", "ic", "fr", "fc")


def halves(v):
    high = v.astype(BF16)
    return high, (v - high.astype(F32)).astype(BF16)


def iota(shape, axis):
    return lax.broadcasted_iota(jnp.int32, shape, axis)


def selector(shape, condition):
    return jnp.where(condition(iota(shape, 0), iota(shape, 1)), 1.0, 0.0).astype(F32)


def exact(a, b, dims):
    return lax.dot_general(a, b, (dims, ((), ())), precision=HIGHEST, preferred_element_type=F32)


def fold(a, b):
    return jnp.dot(a, b, preferred_element_type=F32)


def data_rows(v):
    high, low = halves(v)
    return jnp.concatenate([high, high, low], axis=1)


def data_columns(v):
    high, low = halves(v)
    return jnp.concatenate([high, high, low], axis=0)


def weight_right(v):
    high, low = halves(v)
    return jnp.concatenate([high, low, high], axis=0)


def weight_left(v):
    high, low = halves(v)
    return jnp.concatenate([high, low, high], axis=1)


def kernel(
    coef_size, limb_size, chunks,
    x_ref, zero_ref, km_ref, ks_ref, *rest,
):
    names = len(SMALL)
    sources, (out0_ref, out1_ref) = rest[:names], rest[names:names + 2]
    held, rest = rest[names + 2:2 * names + 2], rest[2 * names + 2:]
    lsem, rest = rest[0], rest[1:]
    loads = {
        name: pltpu.make_async_copy(source, target, lsem.at[n])
        for n, (name, source, target) in enumerate(zip(SMALL, sources, held))
    }
    for name in ("ic", "tim") + tuple(n for n in SMALL if n not in ("ic", "tim")):
        loads[name].start()
    (lift_main_ref, lift_special_ref, lower_ref, scale_ref, tim_ref, tis_ref, tfm_ref, tfs_ref,
     ir_ref, ic_ref, fr_ref, fc_ref) = held
    body(coef_size, limb_size, chunks, loads, x_ref, zero_ref, km_ref, ks_ref,
         lift_main_ref, lift_special_ref, lower_ref, scale_ref, tim_ref, tis_ref, tfm_ref, tfs_ref,
         ir_ref, ic_ref, fr_ref, fc_ref, out0_ref, out1_ref, *rest)


def body(
    coef_size, limb_size, chunks, loads,
    x_ref, zero_ref, km_ref, ks_ref, lift_main_ref, lift_special_ref, lower_ref, scale_ref,
    tim_ref, tis_ref, tfm_ref, tfs_ref, ir_ref, ic_ref, fr_ref, fc_ref,
    out0_ref, out1_ref,
    send1, got1, send2, got2, got3, send_s, got_s, send_m, got_m, send5, got5, send6, got6, got7, send8, got8,
    send_t, got_t, twist, total, ic_w, fc_w, m_w, special_w, main_w, lower_w,
    ssem, rsem, tsem,
):
    coef = lax.axis_index("coef")
    limb = lax.axis_index("limb")
    ring = limb_size // 2
    side = limb // ring
    place = lax.rem(limb, ring)

    barrier = pltpu.get_barrier_semaphore()

    @pl.loop(1, coef_size)
    def _(j):
        pl.semaphore_signal(barrier, inc=1, device_id={"coef": lax.rem(coef + j, coef_size)}, device_id_type=MESH)

    @pl.loop(1, limb_size)
    def _(j):
        pl.semaphore_signal(barrier, inc=1, device_id={"limb": lax.rem(limb + j, limb_size)}, device_id_type=MESH)

    def need(*which):
        for name in which:
            loads[name].wait()

    def push(source, target, axis, peer, stage, g):
        pltpu.make_async_remote_copy(
            src_ref=source, dst_ref=target, send_sem=ssem.at[stage, g], recv_sem=rsem.at[stage, g],
            device_id={axis: peer}, device_id_type=MESH,
        ).start()

    def settle(ref, sem):
        pltpu.make_async_copy(ref, ref, sem).wait()

    tall = coef_size // 4
    chip = coef // 2

    def far_first(j):
        m = j // 4
        odd = lax.rem(m, 2)
        up = odd * (tall // 2 - 1 - m // 2) + (1 - odd) * (tall // 2 + m // 2)
        across = lax.rem(chip // tall + 1 - lax.rem(j // 2, 2), 2)
        return (across * tall + lax.rem(lax.rem(chip, tall) + up, tall)) * 2 + lax.rem(coef + 1 - lax.rem(j, 2), 2)

    def coef_push(send, got, stage, g):
        @pl.loop(0, coef_size - 1)
        def _(j):
            peer = far_first(j)
            push(send.at[g, peer], got.at[g, coef], "coef", peer, stage, g)

        got[g, coef] = send[g, coef]

    def coef_wait(got, stage, g):
        settle(got.at[g, pl.ds(0, coef_size - 1)], rsem.at[stage, g])

    def to_items(ref, g, v):
        for n in range(v.shape[0]):
            for h in range(2):
                ref[g, 2 * n + h] = v[n, :, h * LANE:(h + 1) * LANE]

    def stage1(g):
        v = x_ref[pl.ds(PART * g, PART)].reshape(PART * 2 * SUB, COLS)
        a = fold(data_rows(v), ic_w[...]).reshape(PART, 2, SUB, COLS) * tim_ref[...][None]
        to_items(send1, g, a.reshape(PART * 2, SUB, COLS))

    def push1(g):
        coef_push(send1, got1, 0, g)

    def stage2(g):
        coef_wait(got1, 0, g)
        v = got1[g].reshape(ROWS, LANE)
        send2[g] = fold(m_w[...], data_columns(v)).reshape(coef_size, SUB, LANE)
        coef_push(send2, got2, 1, g)

    def stage3(g):
        coef_wait(got2, 1, g)

        @pl.loop(1, ring)
        def _(j):
            to = lax.rem(place + j, ring)
            push(got2.at[g, pl.ds(4 * to, 4)], got3.at[g, place], "limb", side * ring + to, 2, g)

        got3[g, place] = got2[g, pl.ds(4 * place, 4)]

    def mixed(weight, got, send, per, g):
        v = got[g].reshape(limb_size, 2, SUB, LANE)
        both = jnp.concatenate([v[:, h].reshape(limb_size * SUB, LANE) for h in range(2)], axis=1)
        w = fold(weight[...], data_columns(both)).reshape(limb_size, per, SUB, 2 * LANE)
        for h in range(2):
            send[g, :, :, h] = w[..., h * LANE:(h + 1) * LANE]

    def limb_wait(got, stage, g, count=limb_size - 1):
        settle(got.at[g, pl.ds(0, count)], rsem.at[stage, g])

    def limb_push(send, got, stage, g):
        @pl.loop(1, limb_size)
        def _(j):
            peer = lax.rem(limb + j, limb_size)
            push(send.at[g, peer], got.at[g, limb], "limb", peer, stage, g)

        got[g, limb] = send[g, limb]

    def stage4_special(g):
        limb_wait(got3, 2, g, ring - 1)
        mixed(special_w, got3, send_s, 1, g)
        limb_push(send_s, got_s, 3, g)

    def stage4_main(g):
        mixed(main_w, got3, send_m, 2, g)
        limb_push(send_m, got_m, 8, g)

    def finish(v, scale):
        n, kinds = v.shape[:2]
        parts = [(v[:, :, h] * scale[:, h][None]).reshape(n * kinds * SUB, LANE) for h in range(2)]
        rows = jnp.concatenate(parts, axis=1)
        return fold(data_rows(rows), fc_w[...]).reshape(n, kinds * SUB, COLS)

    def stage5(g):
        limb_wait(got_s, 3, g)
        values = finish(got_s[g], twist[2:]).reshape(2, PART, SUB, COLS)
        here = pl.ds(PART * g, PART)
        special = sum(
            jnp.concatenate([values[d], values[d]], axis=1) * ks_ref[here, d].astype(F32) for d in range(2)
        )
        a = fold(data_rows(special.reshape(PART * 2 * SUB, COLS)), ic_w[...])
        a = a.reshape(PART * 2, SUB, COLS) * tis_ref[...]
        to_items(send5, g, a)
        coef_push(send5, got5, 4, g)

    def stage5_main(g):
        limb_wait(got_m, 8, g)
        values = finish(got_m[g], twist[:2]).reshape(2, PART, 2 * SUB, COLS)
        here = pl.ds(PART * g, PART)
        for i in range(2):
            total[g, :, i] = sum(values[d] * km_ref[here, d, i].astype(F32) for d in range(2))

    def stage6(g):
        coef_wait(got5, 4, g)
        v = got5[g].reshape(ROWS, LANE)
        send6[g] = fold(m_w[...], data_columns(v)).reshape(coef_size, SUB, LANE)
        coef_push(send6, got6, 5, g)

    def stage7(g):
        coef_wait(got6, 5, g)

        @pl.loop(1, limb_size)
        def _(j):
            to = lax.rem(limb + j, limb_size)
            push(got6.at[g, pl.ds(2 * to, 2)], got7.at[g, limb], "limb", to, 6, g)

        got7[g, limb] = got6[g, pl.ds(2 * limb, 2)]

    def stage8(g):
        limb_wait(got7, 6, g)
        mixed(lower_w, got7, send8, 2, g)
        limb_push(send8, got8, 7, g)

    def stage9(g):
        limb_wait(got8, 7, g)
        low = finish(got8[g], twist[:2]).reshape(PART, 2, 2, SUB, COLS)
        here = pl.ds(PART * g, PART)
        for t in range(2):
            for i, out in enumerate((out0_ref, out1_ref)):
                result = scale_ref[t] * (total[g, :, i, t * SUB:(t + 1) * SUB] - low[:, i, t])
                out[here, t] = zero_ref[here, t] + result if i == 0 else result

    def prepare_twist():
        rows = jnp.concatenate(
            [tfm_ref[...].reshape(2 * SUB, ROWS), tfs_ref[...].reshape(SUB, ROWS), jnp.zeros((LANE - 3 * SUB, ROWS), F32)],
            axis=0,
        )
        send_t[...] = rows.T.reshape(coef_size, SUB, LANE)

    def push_twist():
        @pl.loop(1, coef_size)
        def _(j):
            peer = lax.rem(coef + j, coef_size)
            pltpu.make_async_remote_copy(
                src_ref=send_t.at[peer], dst_ref=got_t.at[coef], send_sem=tsem.at[0], recv_sem=tsem.at[1],
                device_id={"coef": peer}, device_id_type=MESH,
            ).start()

        got_t[coef] = send_t[coef]

    def build_twist():
        settle(got_t.at[pl.ds(0, coef_size - 1)], tsem.at[1])
        lanes = iota((SUB, LANE), 1) // SUB
        per = LANE // SUB
        for t in range(3):
            for h in range(2):
                value = jnp.zeros((SUB, LANE), F32)
                for q in range(per):
                    tile = got_t[h * per + q]
                    shift = (q - t) * SUB % LANE
                    moved = pltpu.roll(tile, shift, 1) if shift else tile
                    value = jnp.where(lanes == q, moved, value)
                twist[t, h] = value

    def build_weights():
        m_w[...] = weight_left(exact(fr_ref[...], ir_ref[...], ((0,), (1,))))
        fc_w[...] = weight_right(fc_ref[...])

    def build_mixes():
        depth = limb_size * SUB
        kinds = limb_size * 2

        def expand(table, spread):
            rows = table.shape[0]
            wide = exact(table, spread, ((1,), (0,)))
            keep = lax.rem(iota((rows, depth), 0), SUB) == lax.rem(iota((rows, depth), 1), SUB)
            return weight_left(jnp.where(keep, wide, 0.0))

        pick = selector((kinds * SUB, kinds), lambda r, t: r // SUB == t)
        mine = selector((kinds, depth), lambda s, c: c // SUB + side * limb_size == s)
        table = exact(selector((depth, limb_size), lambda r, u: r // SUB == u), lift_special_ref[...], ((1,), (0,)))
        special_w[...] = expand(table, mine)
        main_w[...] = expand(exact(pick, lift_main_ref[...], ((1,), (1,))), mine)
        table = exact(pick, lower_ref[...], ((1,), (1,)))
        lower_w[...] = expand(table, selector((limb_size, depth), lambda s, c: c // SUB == s))

    every = range(chunks)
    need("ic", "tim")
    ic_w[...] = weight_right(ic_ref[...])
    for g in every:
        stage1(g)
    pl.semaphore_wait(barrier, coef_size + limb_size - 2)
    for g in every:
        push1(g)
    need("ir", "fr", "fc", "tfm", "tfs", "tis", "scale", "lift_main", "lift_special", "lower")
    build_weights()
    build_mixes()
    prepare_twist()
    for g in every:
        stage2(g)
    for g in every:
        stage3(g)
    push_twist()
    for step in (stage4_special, stage4_main):
        for g in every:
            step(g)
    build_twist()
    for step in (stage5, stage6, stage7, stage8, stage5_main, stage9):
        for g in every:
            step(g)

    for g in range(chunks):
        for stage, ref, count in (
            (0, got1, coef_size - 1), (1, got2, coef_size - 1), (2, got3, ring - 1), (3, got_s, limb_size - 1), (8, got_m, limb_size - 1),
            (4, got5, coef_size - 1), (5, got6, coef_size - 1), (6, got7, limb_size - 1), (7, got8, limb_size - 1),
        ):
            settle(ref.at[g, pl.ds(0, count)], ssem.at[stage, g])
    settle(got_t.at[pl.ds(0, coef_size - 1)], tsem.at[0])


def on_device(
    coef_size, limb_size,
    cipher_zero, cipher_one, key_main, key_special, lift_main, lift_special, lower_table, inverse_scale,
    inverse_main, inverse_special, forward_main, forward_special,
    inverse_rows, inverse_columns, forward_rows, forward_columns,
):
    ciphers = cipher_one.shape[0]
    chunks = ciphers // PART
    tile = (SUB, LANE)
    vmem = pl.BlockSpec(memory_space=pltpu.VMEM)
    small = (
        lift_main, lift_special.T, lower_table, inverse_scale, inverse_main, inverse_special, forward_main, forward_special,
        inverse_rows, inverse_columns, forward_rows, forward_columns,
    )
    out = jax.ShapeDtypeStruct((ciphers, 2, SUB, COLS), F32)
    item = pltpu.VMEM((chunks, coef_size) + tile, F32)
    depth = limb_size * SUB
    stages = 9
    zero, one = pl.pallas_call(
        functools.partial(kernel, coef_size, limb_size, chunks),
        out_shape=(out, out),
        in_specs=[vmem] * 4 + [pl.BlockSpec(memory_space=pltpu.HBM)] * len(small),
        out_specs=(vmem, vmem),
        scratch_shapes=[
            *(pltpu.SMEM(v.shape, F32) if v.ndim == 1 else pltpu.VMEM(v.shape, F32) for v in small),
            pltpu.SemaphoreType.DMA((len(small),)),
            item, item, item, item,
            pltpu.VMEM((chunks, limb_size // 2, 4) + tile, F32),
            pltpu.VMEM((chunks, limb_size, 1, 2) + tile, F32),
            pltpu.VMEM((chunks, limb_size, 1, 2) + tile, F32),
            pltpu.VMEM((chunks, limb_size, 2, 2) + tile, F32),
            pltpu.VMEM((chunks, limb_size, 2, 2) + tile, F32),
            item, item, item, item,
            pltpu.VMEM((chunks, limb_size, 2) + tile, F32),
            pltpu.VMEM((chunks, limb_size, 2, 2) + tile, F32),
            pltpu.VMEM((chunks, limb_size, 2, 2) + tile, F32),
            pltpu.VMEM((coef_size,) + tile, F32),
            pltpu.VMEM((coef_size,) + tile, F32),
            pltpu.VMEM((3, 2) + tile, F32),
            pltpu.VMEM((chunks, PART, 2, 2 * SUB, COLS), F32),
            pltpu.VMEM((3 * COLS, COLS), BF16),
            pltpu.VMEM((3 * COLS, COLS), BF16),
            pltpu.VMEM((ROWS, 3 * ROWS), BF16),
            pltpu.VMEM((depth, 3 * depth), BF16),
            pltpu.VMEM((2 * depth, 3 * depth), BF16),
            pltpu.VMEM((2 * depth, 3 * depth), BF16),
            pltpu.SemaphoreType.DMA((stages, chunks)),
            pltpu.SemaphoreType.DMA((stages, chunks)),
            pltpu.SemaphoreType.DMA((2,)),
        ],
        compiler_params=pltpu.CompilerParams(
            collective_id=0, has_side_effects=True, vmem_limit_bytes=40 << 20
        ),
    )(
        cipher_one.reshape(ciphers, 2, SUB, COLS),
        cipher_zero.reshape(ciphers, 2, SUB, COLS),
        key_main.reshape(ciphers, 2, 2, 2 * SUB, COLS),
        key_special.reshape(ciphers, 2, 2 * SUB, COLS),
        *(pltpu.with_memory_space_constraint(v, pltpu.HBM) for v in small),
    )
    return zero.reshape(cipher_zero.shape), one.reshape(cipher_one.shape)


def solution(mesh):
    spread = P(None, "limb", "coef")
    keys = P(None, None, None, "limb", "coef")
    local = P("limb", "coef", None)
    placed = (spread, spread, keys, keys, P(), P(), P(), P("limb"), local, local, local, local, P(), P(), P(), P())
    return jax.shard_map(
        functools.partial(on_device, mesh.shape["coef"], mesh.shape["limb"]),
        mesh=mesh,
        in_specs=placed,
        out_specs=(spread, spread),
        check_vma=False,
    )
```
